256 devices in a mesh: row: 32 (over z_lo, y, x), col: 8 (over z_hi, core).
Axes of the slice: x: 4, y: 4, z: 8 (z_hi: 4, z_lo: 2; z = z_hi * 2 + z_lo), core: 2. Of those that a mesh axis runs over, the one named last changes fastest.
Arguments:
- c_left: float32 [32, 8, 2048, 256], P('row', 'col'), may hold values from -6 to 6
- c_right: float32 [32, 8, 2048, 256], P('row', 'col'), may hold values from -6 to 6
- c_rank: int32 [32, 8], P('row', 'col'), may hold values from 32 to 256, as said below
- a_left: bfloat16 [32, 2, 2048, 256], P('row', None, 'col'), may hold values from -6 to 6
- a_right: bfloat16 [32, 2, 2048, 256], P('row', None, 'col'), may hold values from -0.125 to 0.125
- a_rank: int32 [32, 2], P('row'), may hold values from 32 to 256, as said below
- a_pattern: int32 [32, 2], P('row'), may hold values 0 or 1
- b_left: bfloat16 [2, 8, 2048, 256], P(None, 'col', 'row'), may hold values from -6 to 6
- b_right: bfloat16 [2, 8, 2048, 256], P(None, 'col', 'row'), may hold values from -0.375 to 0.375
- b_rank: int32 [2, 8], P(None, 'col'), may hold values from 32 to 256, as said below
- b_pattern: int32 [2, 8], P(None, 'col'), may hold values 0 or 1
- probe: bfloat16 [2, 2048, 256], replicated, may hold values from -6 to 6
- target: int32 [32, 8, 2], P('row', 'col'), may hold values from 16 to 240, as said below
Outputs:
- out_left: float32 [32, 8, 2048, 256], P('row', 'col')
- out_right: float32 [32, 8, 2048, 256], P('row', 'col')
The draws below stay inside these ranges and needn't reach their ends.
Inputs may be any that keep to these rules, and one draw needn't show every extreme that they name: `c_rank`: every rank lies from 32 to 256; both ends are taken by some tile. `a_rank`: every rank lies from 32 to 256; both ends are taken by some tile. `b_rank`: every rank lies from 32 to 256; both ends are taken by some tile. With g(r) = max(8, r // 16): target[i, j, 0] <= c_rank[i, j] - g(c_rank[i, j]) and target[i, j, k] <= target[i, j, k - 1] - g(target[i, j, k - 1]); both ends are taken by some tile.
All inputs are finite; a program needn't handle non-finite values. No bound on the sum of `a_pattern` or of `b_pattern` on one device may be relied on, other than what follows from the above.
Results may differ from the reference program's by a relative error of at most 0.0009.
Values may be sent and summed in bfloat16 or wider, within the bound.
A program may use at most 128 MiB of HBM per device.

```python
import math
import jax
import jax.numpy as jnp
from jax import lax

NB = 2048
R = 256
RMIN = 32
KS = 2
MT = 32
NT = 8


def ranks_with_ends(key, count):
    first, second = jax.random.split(key)
    values = jax.random.randint(first, (count,), RMIN, R + 1)
    order = jax.random.permutation(second, count)
    places = jnp.arange(count)
    values = jnp.where(places == order[0], R, values)
    values = jnp.where(places == order[1], RMIN, values)
    return (values, order)


def margin_of(ranks):
    return jnp.maximum(RMIN // 4, ranks // 16)


def rank_table(key):
    base = jax.random.fold_in(key, 11)
    count = MT * NT
    c_values, order = ranks_with_ends(base, count)
    places = jnp.arange(count)
    columns = []
    previous = c_values
    for step in range(KS):
        step_key = jax.random.fold_in(base, 100 + step)
        lowest = RMIN // 2 + (KS - 1 - step) * (RMIN // 4)
        highest = jnp.maximum(previous - margin_of(previous), lowest)
        chosen = lowest + jax.random.randint(step_key, (count,), 0, highest - lowest + 1)
        chosen = jnp.where(places == order[0], highest, chosen)
        chosen = jnp.where(places == order[1], lowest, chosen)
        columns.append(chosen)
        previous = chosen
    return (c_values.reshape(MT, NT).astype(jnp.int32), jnp.stack(columns, -1).reshape(MT, NT, KS).astype(jnp.int32))


def draw_c_rank(key, part):
    return rank_table(key)[0]


def draw_target(key, part):
    return rank_table(key)[1]


def draw_a_rank(key, part):
    values, order = ranks_with_ends(jax.random.fold_in(key, 23), MT * KS)
    return values.reshape(MT, KS).astype(jnp.int32)


def draw_b_rank(key, part):
    values, order = ranks_with_ends(jax.random.fold_in(key, 37), KS * NT)
    return values.reshape(KS, NT).astype(jnp.int32)


def touch_ends(array, stream_key, least, largest):
    extent = array.shape
    place = [jax.random.randint(jax.random.fold_in(stream_key, axis), (), 0, extent[axis]) for axis in range(len(extent))]
    array = array.at[tuple(place)].set(least)
    longest = extent.index(max(extent))
    place[longest] = (place[longest] + 1) % extent[longest]
    return array.at[tuple(place)].set(largest)


def shard_levels(stream_key, dims, shards, low, top_value):
    level, own = 1.0, jax.random.fold_in(stream_key, 6)
    for axis_at, shards_of in shards:
        draws = jnp.exp(jax.random.uniform(jax.random.fold_in(own, axis_at), (shards_of,), jnp.float32, low / len(shards), top_value / len(shards)))
        level = level * jnp.repeat(draws, dims[axis_at] // shards_of).reshape([-1 if axis == axis_at else 1 for axis in range(len(dims))])
    return level


def noise(stream_key, extent, spread, reach, cuts=(), kind=jnp.bfloat16):
    array = jax.random.normal(stream_key, extent, jnp.float32) * spread
    if len(cuts) > 0:
        array = shard_levels(stream_key, extent, cuts, -0.22, 0.18) * array
    return jnp.clip(array, min=-reach, max=reach).astype(kind)


def setup_inputs(seed: int = 0) -> dict:
    keys = jax.random.split(jax.random.key(seed), 14)
    c_left = noise(keys[0], (MT, NT, NB, R), 1.0, 6.0, ((0, 32), (1, 8)), jnp.float32)
    c_right = noise(keys[1], (MT, NT, NB, R), 1.0, 6.0, ((0, 32), (1, 8)), jnp.float32)
    c_rank = draw_c_rank(jax.random.fold_in(keys[13], 71), 0)
    a_left = noise(keys[3], (MT, KS, NB, R), 1.0, 6.0, ((0, 32), (2, 8)))
    a_right = noise(keys[4], (MT, KS, NB, R), NB ** -0.5, 0.125, ((0, 32), (2, 8)))
    a_rank = draw_a_rank(jax.random.fold_in(keys[13], 71), 0)
    a_pattern = touch_ends((jax.random.randint(keys[6], (MT, KS), 0, 4) < 3).astype(jnp.int32), jax.random.fold_in(keys[6], 1), 0, 1)
    b_left = noise(keys[7], (KS, NT, NB, R), 1.0, 6.0, ((1, 8), (2, 32)))
    b_right = noise(keys[8], (KS, NT, NB, R), R ** -0.5, 0.375, ((1, 8), (2, 32)))
    b_rank = draw_b_rank(jax.random.fold_in(keys[13], 71), 0)
    b_pattern = touch_ends((jax.random.randint(keys[10], (KS, NT), 0, 4) < 3).astype(jnp.int32), jax.random.fold_in(keys[10], 1), 0, 1)
    probe = noise(keys[11], (KS, NB, R), 1.0, 6.0)
    target = draw_target(jax.random.fold_in(keys[13], 71), 0)
    return {"c_left": c_left, "c_right": c_right, "c_rank": c_rank, "a_left": a_left, "a_right": a_right, "a_rank": a_rank, "a_pattern": a_pattern, "b_left": b_left, "b_right": b_right, "b_rank": b_rank, "b_pattern": b_pattern, "probe": probe, "target": target}


def column_mask(count, width):
    return (jnp.arange(width, dtype=jnp.int32) < count).astype(jnp.float32)

def product_of(left, right):
    return jnp.dot(left.astype(jnp.float32), right.astype(jnp.float32), precision=lax.Precision.HIGHEST, preferred_element_type=jnp.float32)

def transposed_product(left, right):
    return lax.dot_general(left.astype(jnp.float32), right.astype(jnp.float32), (((0,), (0,)), ((), ())), precision=lax.Precision.HIGHEST, preferred_element_type=jnp.float32)

def recompress(left, right, keep, extra, extra_right, right_probe, probe_step, tmask):
    tile = left.shape[0]
    probe_cols = probe_step.astype(jnp.float32) * tmask[None, :]
    core_c = transposed_product(right, probe_cols) * keep[:, None]
    core_b = right_probe * tmask[None, :]
    sample = product_of(left, core_c) + product_of(extra, core_b)
    gram = transposed_product(sample, sample) + jnp.diag(1.0 - tmask)
    factor = jnp.linalg.cholesky(gram)
    basis = lax.linalg.triangular_solve(factor, sample, left_side=False, lower=True, transpose_a=True)
    back_c = transposed_product(left, basis) * keep[:, None]
    back_b = transposed_product(extra, basis)
    new_right = (product_of(right, back_c) + product_of(extra_right, back_b)) / math.sqrt(tile)
    return (basis * math.sqrt(tile), new_right)

def reference(c_left, c_right, c_rank, a_left, a_right, a_rank, a_pattern, b_left, b_right, b_rank, b_pattern, probe, target):

    def one_tile(index):
        row_id = index // NT
        col_id = index % NT
        left = c_left[row_id, col_id]
        right = c_right[row_id, col_id]
        keep = column_mask(c_rank[row_id, col_id], R)
        for step in range(KS):
            a_l = a_left[row_id, step]
            a_r = a_right[row_id, step]
            b_l = b_left[step, col_id]
            b_r = b_right[step, col_id]
            weight = (a_pattern[row_id, step] * b_pattern[step, col_id]).astype(jnp.float32)
            middle = lax.dot_general(a_r.astype(jnp.float32), b_l.astype(jnp.float32), (((0,), (0,)), ((), ())), preferred_element_type=jnp.float32)
            middle = middle * column_mask(a_rank[row_id, step], R)[:, None] * column_mask(b_rank[step, col_id], R)[None, :] * weight
            extra = product_of(a_l.astype(jnp.float32), middle)
            right_probe = lax.dot_general(b_r.astype(jnp.float32), probe[step].astype(jnp.float32), (((0,), (0,)), ((), ())), preferred_element_type=jnp.float32)
            tmask = column_mask(target[row_id, col_id, step], R)
            left, right = recompress(left, right, keep, extra, b_r.astype(jnp.float32), right_probe, probe[step], tmask)
            keep = tmask
        return (left, right)
    lefts, rights = lax.map(one_tile, jnp.arange(MT * NT, dtype=jnp.int32))
    return (lefts.reshape(MT, NT, NB, R), rights.reshape(MT, NT, NB, R))
```

```python
import functools
import math

import jax
import jax.numpy as jnp
from jax import lax
from jax.experimental import pallas as pl
from jax.experimental.pallas import tpu as pltpu
from jax.sharding import PartitionSpec as P

F32 = jnp.float32
BF16 = jnp.bfloat16
PANEL = 32
CHUNK = 256


def split2(x):
    hi = x.astype(BF16)
    return hi, (x - hi.astype(F32)).astype(BF16)


def split3(x):
    hi = x.astype(BF16)
    rest = x - hi.astype(F32)
    mid = rest.astype(BF16)
    return hi, mid, (rest - mid.astype(F32)).astype(BF16)


def mm(a, b):
    return jnp.dot(a, b, preferred_element_type=F32)


def tmm(a, b):
    return lax.dot_general(a, b, (((0,), (0,)), ((), ())), preferred_element_type=F32)


def mmt(a, b):
    return lax.dot_general(a, b, (((1,), (1,)), ((), ())), preferred_element_type=F32)


def times(op, a, b):
    ah, al = split2(a)
    bh, bl = split2(b)
    return op(ah, bh) + (op(ah, bl) + op(al, bh))


def fine(op, a, b):
    a0, a1, a2 = split3(a)
    b0, b1, b2 = split3(b)
    return op(a0, b0) + ((op(a0, b1) + op(a1, b0)) + (op(a1, b1) + (op(a0, b2) + op(a2, b0))))


def lane(x, c):
    return jnp.broadcast_to(x[:, c : c + 1], (8, 128))


def sublane(x, r):
    return jnp.broadcast_to(x[r : r + 1, :], (8, 128))


def panel_step(p, work, inv_ref):
    width = work.shape[1] // 2
    vregs = work.shape[1] // 128
    groups = PANEL // 8
    rows = [
        [work[8 * g : 8 * g + 8, 128 * v : 128 * v + 128] for v in range(vregs)] for g in range(groups)
    ]
    below = pltpu.roll(work[PANEL:width, :width], width - PANEL, 1)
    sub = lax.broadcasted_iota(jnp.int32, (8, 128), 0)
    for b in range(groups):
        cols = [[lane(rows[g][0], 8 * b + m) for m in range(8)] for g in range(groups)]
        d = [[sublane(cols[b][n], m) for n in range(m + 1)] for m in range(8)]
        heads = [[sublane(rows[b][v], n) for v in range(vregs)] for n in range(8)]
        w = [[None] * 8 for _ in range(8)]
        low = [[None] * 8 for _ in range(8)]
        for k in range(8):
            r = lax.rsqrt(d[k][k])
            w[k][k] = r
            for m in range(k + 1, 8):
                low[m][k] = d[m][k] * r
            for m in range(k + 1, 8):
                for n in range(k + 1, m + 1):
                    d[m][n] = d[m][n] - low[m][k] * low[n][k]
            for n in range(k):
                total = low[k][n] * w[n][n]
                for l in range(n + 1, k):
                    total = total + low[k][l] * w[l][n]
                w[k][n] = -(total * r)
        for v in range(vregs):
            total = None
            for n in range(8):
                column = jnp.zeros((8, 128), F32)
                for m in range(n, 8):
                    column = jnp.where(sub == m, w[m][n], column)
                term = column * heads[n][v]
                total = term if total is None else total + term
            rows[b][v] = total
        for g in range(b + 1, groups):
            heads_u = [[sublane(rows[b][v], m) for v in range(vregs)] for m in range(8)]
            for m in range(8):
                coef = w[m][0] * cols[g][0]
                for l in range(1, m + 1):
                    coef = coef + w[m][l] * cols[g][l]
                for v in range(vregs):
                    rows[g][v] = rows[g][v] - coef * heads_u[m][v]
    upper = jnp.concatenate([jnp.concatenate(rows[g], axis=1) for g in range(groups)], axis=0)
    start = pl.multiple_of(p * PANEL, PANEL)
    inv_ref[pl.ds(start, PANEL), :] = upper[:, width:]
    ahead = pltpu.roll(upper[:, :width], width - PANEL, 1)
    h, m, l = split3(jnp.concatenate([ahead, upper[:, width:]], axis=1))
    hg, mg, lg = h[:, :width], m[:, :width], l[:, :width]
    update = tmm(
        jnp.concatenate([hg, hg, mg, mg, hg, lg], axis=0),
        jnp.concatenate([h, m, h, m, l, h], axis=0),
    )
    rest = width - PANEL
    work[0:rest, width:] = work[PANEL:width, width:] - update[:rest, width:]
    work[0:rest, :width] = below - update[:rest, :width]


def inverse_factor(gram, live, work, inv_ref):
    width = gram.shape[0]
    r = lax.broadcasted_iota(jnp.int32, (width, width), 0)
    c = lax.broadcasted_iota(jnp.int32, (width, width), 1)
    eye = jnp.where(r == c, 1.0, 0.0)
    work[:, :width] = gram + eye * (1.0 - live)
    work[:, width:] = eye

    def body(p, carry):
        panel_step(p, work, inv_ref)
        return carry

    lax.fori_loop(0, width // PANEL, body, 0)


def compute_kernel(
    ranks,
    left,
    right,
    probe,
    al,
    ar,
    bl,
    br,
    out_left,
    out_right,
    work,
    inv0,
    inv1,
    s0h,
    s0l,
    s1h,
    s1l,
):
    tile, width = left.shape
    chunks = tile // CHUNK
    crank, t0, t1 = ranks[0], ranks[1], ranks[2]
    lanes = lax.broadcasted_iota(jnp.int32, (1, width), 1)
    subs = lax.broadcasted_iota(jnp.int32, (width, 1), 0)

    def row_mask(count):
        return jnp.where(subs < count, 1.0, 0.0).astype(F32)

    def lane_mask(count):
        return jnp.where(lanes < count, 1.0, 0.0).astype(F32)

    keep = row_mask(crank)
    live0, live1 = lane_mask(t0), lane_mask(t1)
    zero = jnp.zeros((width, width), F32)

    def at(i):
        return pl.ds(pl.multiple_of(i * CHUNK, CHUNK), CHUNK)

    def before(i, carry):
        rp0, rp1 = carry
        rh, rl = split2(right[at(i), :])
        p0, p1 = probe[0, at(i), :], probe[1, at(i), :]
        return rp0 + (tmm(rh, p0) + tmm(rl, p0)), rp1 + (tmm(rh, p1) + tmm(rl, p1))

    core0, rp1 = lax.fori_loop(0, chunks, before, (zero, zero))
    core0 = core0 * keep * live0
    rp1 = rp1 * keep

    def cores(i, carry):
        m0, m1, b00, b01, b11 = carry
        x0, x1 = br[0, at(i), :], br[1, at(i), :]
        p0, p1 = probe[0, at(i), :], probe[1, at(i), :]
        return (
            m0 + tmm(ar[0, at(i), :], bl[0, at(i), :]),
            m1 + tmm(ar[1, at(i), :], bl[1, at(i), :]),
            b00 + tmm(x0, p0),
            b01 + tmm(x0, p1),
            b11 + tmm(x1, p1),
        )

    mid0, mid1, b00, b01, b11 = lax.fori_loop(0, chunks, cores, (zero,) * 5)
    weight0, weight1 = ranks[7].astype(F32), ranks[8].astype(F32)
    mid0 = mid0 * row_mask(ranks[3]) * lane_mask(ranks[5]) * weight0
    mid1 = mid1 * row_mask(ranks[4]) * lane_mask(ranks[6]) * weight1
    sc0 = fine(mm, mid0, b00) * live0
    sc1 = fine(mm, mid1, b11) * live1

    core0h, core0l = split2(core0)
    sc0h, sc0l = split2(sc0)

    def first(i, carry):
        gh, gx, gl, ls, as_ = carry
        lh, ll = split2(left[at(i), :])
        a = al[0, at(i), :]
        s = (mm(lh, core0h) + (mm(lh, core0l) + mm(ll, core0h))) + (mm(a, sc0h) + mm(a, sc0l))
        sh, sl = split2(s)
        s0h[at(i), :] = sh
        s0l[at(i), :] = sl
        return (
            gh + tmm(sh, sh),
            gx + tmm(sh, sl),
            gl + tmm(sl, sl),
            ls + (tmm(lh, sh) + (tmm(lh, sl) + tmm(ll, sh))),
            as_ + (tmm(a, sh) + tmm(a, sl)),
        )

    gh, gx, gl, ls0, as0 = lax.fori_loop(0, chunks, first, (zero,) * 5)
    inverse_factor(gh + (gx + gx.T) + gl, live0, work, inv0)
    w0 = inv0[...]

    y = fine(tmm, ls0, rp1) + fine(tmm, as0, fine(mm, mid0, b01))
    z = fine(tmm, w0, fine(mm, w0, y)) * live1
    zh, zl = split2(z)
    sc1h, sc1l = split2(sc1)

    def second(i, carry):
        gh, gx, gl, ss, as_ = carry
        a = al[1, at(i), :]
        ph, pl_ = s0h[at(i), :], s0l[at(i), :]
        s = (mm(ph, zh) + (mm(ph, zl) + mm(pl_, zh))) + (mm(a, sc1h) + mm(a, sc1l))
        sh, sl = split2(s)
        s1h[at(i), :] = sh
        s1l[at(i), :] = sl
        return (
            gh + tmm(sh, sh),
            gx + tmm(sh, sl),
            gl + tmm(sl, sl),
            ss + (tmm(ph, sh) + (tmm(ph, sl) + tmm(pl_, sh))),
            as_ + (tmm(a, sh) + tmm(a, sl)),
        )

    gh, gx, gl, ss, as1 = lax.fori_loop(0, chunks, second, (zero,) * 5)
    inverse_factor(gh + (gx + gx.T) + gl, live1, work, inv1)
    w1 = inv1[...]

    root = math.sqrt(tile)
    turn = fine(mmt, fine(mm, w0, ss), w1)
    hold = fine(mmt, ls0, w0) * keep
    tr = fine(mm, hold, turn) * (1.0 / root)
    tb0 = fine(tmm, mid0, fine(mm, fine(mmt, as0, w0), turn)) * (1.0 / root)
    tb1 = fine(tmm, mid1, fine(mmt, as1, w1)) * (1.0 / root)
    w1h, w1l = split2(w1 * root)
    trh, trl = split2(tr)
    tb0h, tb0l = split2(tb0)
    tb1h, tb1l = split2(tb1)

    def last(i, carry):
        sh, sl = s1h[at(i), :], s1l[at(i), :]
        out_left[at(i), :] = mmt(sh, w1h) + (mmt(sh, w1l) + mmt(sl, w1h))
        rh, rl = split2(right[at(i), :])
        x0, x1 = br[0, at(i), :], br[1, at(i), :]
        out_right[at(i), :] = (mm(rh, trh) + (mm(rh, trl) + mm(rl, trh))) + (
            (mm(x0, tb0h) + mm(x0, tb0l)) + (mm(x1, tb1h) + mm(x1, tb1l))
        )
        return carry

    lax.fori_loop(0, chunks, last, 0)


def compute(ranks, left, right, probe, al, ar, bl, br):
    tile, width = left.shape
    vmem = pl.BlockSpec(memory_space=pltpu.VMEM)
    return pl.pallas_call(
        compute_kernel,
        out_shape=[jax.ShapeDtypeStruct((tile, width), F32)] * 2,
        in_specs=[pl.BlockSpec(memory_space=pltpu.SMEM)] + [vmem] * 7,
        out_specs=[vmem] * 2,
        scratch_shapes=[
            pltpu.VMEM((width, 2 * width), F32),
            pltpu.VMEM((width, width), F32),
            pltpu.VMEM((width, width), F32),
        ]
        + [pltpu.VMEM((tile, width), BF16)] * 4,
        compiler_params=pltpu.CompilerParams(vmem_limit_bytes=60 * 1024 * 1024),
    )(ranks, left, right, probe, al, ar, bl, br)


class Exchange:
    COPIES = 40

    def __init__(self, k, al_in, ar_in, bl_in, br_in, al, ar, bl, br, send, recv, local):
        self.k = k
        self.send, self.recv, self.local = send, recv, local
        row, col = lax.axis_index("row"), lax.axis_index("col")
        self.x, self.y, self.z = row % 4, (row // 4) % 4, row // 16
        self.h, self.c = col // 2, col % 2
        self.row, self.col = row, col
        self.ins = {"al": al_in, "ar": ar_in, "bl": bl_in, "br": br_in}
        self.full = {"al": al, "ar": ar, "bl": bl, "br": br}
        self.base = k * self.COPIES
        self.offset = {"bl": 0, "br": 11, "ar": 22, "al": 31}

    def at_row(self, x=None, y=None, z=None):
        x = self.x if x is None else x
        y = self.y if y is None else y
        z = self.z if z is None else z
        return ((z * 4 + y) * 4 + x, self.col)

    def at_col(self, h=None, c=None):
        h = self.h if h is None else h
        c = self.c if c is None else c
        return (self.row, h * 2 + c)

    def peers(self):
        yield self.at_row(z=1 - self.z)
        for d in (1, 2, 3):
            yield self.at_row(x=(self.x + d) % 4)
            yield self.at_row(y=(self.y + d) % 4)
        yield self.at_col(h=(self.h + 1) % 4)
        yield self.at_col(h=(self.h + 3) % 4)
        yield self.at_col(c=1 - self.c)

    def copy(self, name, i, src, dst, to):
        n = self.base + self.offset[name] + i
        return pltpu.make_async_remote_copy(
            src_ref=src,
            dst_ref=dst,
            send_sem=self.send.at[n],
            recv_sem=self.recv.at[n],
            device_id=to,
            device_id_type=pl.DeviceIdType.MESH,
        )

    def own(self, name):
        i = ("bl", "br", "ar", "al").index(name)
        src = self.ins[name].at[self.k]
        dst = self.full[name].at[self.k]
        dst = dst.at[self.z, self.y, self.x] if name[0] == "b" else dst.at[self.h, self.c]
        return pltpu.make_async_copy(src, dst, self.local.at[4 * self.k + i])

    def b_pair(self, name):
        src = self.ins[name].at[self.k]
        full = self.full[name].at[self.k]
        return [self.copy(name, 0, src, full.at[self.z, self.y, self.x], self.at_row(z=1 - self.z))]

    def b_near(self, name, second):
        full = self.full[name].at[self.k]
        z = 1 - self.z if second else self.z
        slot = full.at[z, self.y, self.x]
        src = slot if second else self.ins[name].at[self.k]
        out = []
        for d in (1, 2, 3):
            to = self.at_row(x=(self.x + d) % 4) if name == "bl" else self.at_row(y=(self.y + d) % 4)
            out.append(self.copy(name, (3 if second else 0) + d, src, slot, to))
        return out

    def b_line(self, name, place, z=None):
        full = self.full[name].at[self.k]
        if name == "bl":
            return full.at[:, place] if z is None else full.at[z, place]
        return full.at[:, :, place] if z is None else full.at[z, :, place]

    def b_to(self, name, step):
        if name == "bl":
            return self.at_row(y=(self.y + step) % 4)
        return self.at_row(x=(self.x + step) % 4)

    def b_far(self, name):
        here = self.y if name == "bl" else self.x
        line = self.b_line(name, here)
        return [self.copy(name, 7, line, line, self.b_to(name, 1)), self.copy(name, 8, line, line, self.b_to(name, 3))]

    def b_last(self, name):
        here = self.y if name == "bl" else self.x
        back = self.b_line(name, (here + 3) % 4, 0)
        ahead = self.b_line(name, (here + 1) % 4, 1)
        return [self.copy(name, 9, back, back, self.b_to(name, 1)), self.copy(name, 10, ahead, ahead, self.b_to(name, 3))]

    def a_slot(self, name, h, half=None):
        slot = self.full[name].at[self.k].at[h, self.c]
        if half is None:
            return slot
        n = slot.shape[0] // 2
        return slot.at[pl.ds(half * n, n)]

    def a_first(self, name):
        src = self.ins[name].at[self.k]
        slot = self.a_slot(name, self.h)
        return [
            self.copy(name, 0, src, slot, self.at_col(h=(self.h + 1) % 4)),
            self.copy(name, 1, src, slot, self.at_col(h=(self.h + 3) % 4)),
            self.copy(name, 4, src, slot, self.at_col(c=1 - self.c)),
        ]

    def a_second(self, name):
        back = self.a_slot(name, (self.h + 3) % 4, 0)
        ahead = self.a_slot(name, (self.h + 1) % 4, 1)
        return [
            self.copy(name, 2, back, back, self.at_col(h=(self.h + 1) % 4)),
            self.copy(name, 3, ahead, ahead, self.at_col(h=(self.h + 3) % 4)),
        ]

    def a_core(self, name):
        out = []
        for i, d in ((5, 3), (6, 1)):
            slot = self.a_slot(name, (self.h + d) % 4)
            out.append(self.copy(name, i, slot, slot, self.at_col(c=1 - self.c)))
        return out

    def a_core_last(self, name):
        out = []
        for half in (0, 1):
            slot = self.a_slot(name, (self.h + 2) % 4, half)
            out.append(self.copy(name, 7 + half, slot, slot, self.at_col(c=1 - self.c)))
        return out


def start(copies):
    for c in copies:
        c.start()
    return copies


def landed(copies):
    for c in copies:
        c.wait_recv()


def left_here(copies):
    for c in copies:
        c.wait_send()


def greet(exchange):
    barrier = pltpu.get_barrier_semaphore()
    count = 0
    for peer in exchange.peers():
        pl.semaphore_signal(barrier, inc=1, device_id=peer, device_id_type=pl.DeviceIdType.MESH)
        count += 1
    pl.semaphore_wait(barrier, count)


def gather_kernel(al_in, ar_in, bl_in, br_in, al, ar, bl, br, send, recv, local):
    steps = [
        Exchange(k, al_in, ar_in, bl_in, br_in, al, ar, bl, br, send, recv, local) for k in range(2)
    ]
    owns = [e.own(n) for e in steps for n in ("bl", "br", "ar", "al")]
    start(owns)
    greet(steps[0])
    flown = []

    def go(copies):
        flown.extend(copies)
        return start(copies)

    for c in owns:
        c.wait()
    for e in steps:
        pair = {n: go(e.b_pair(n)) for n in ("bl", "br")}
        near = {n: go(e.b_near(n, False)) for n in ("bl", "br")}
        first = {n: go(e.a_first(n)) for n in ("ar", "al")}
        second = {}
        for n in ("bl", "br"):
            landed(pair[n])
            near[n] = near[n] + go(e.b_near(n, True))
        far = {}
        for n in ("bl", "br"):
            landed(near[n])
            far[n] = go(e.b_far(n))
        for n in ("ar", "al"):
            landed(first[n])
            second[n] = go(e.a_second(n))
            first[n] = go(e.a_core(n))
        last = {}
        for n in ("bl", "br"):
            landed(far[n])
            last[n] = go(e.b_last(n))
        for n in ("ar", "al"):
            landed(second[n])
            second[n] = go(e.a_core_last(n))
        for n in ("bl", "br"):
            landed(last[n])
        for n in ("ar", "al"):
            landed(first[n])
            landed(second[n])
    left_here(flown)


def gather(al, ar, bl, br):
    steps, _, width = al.shape
    hbm = pl.BlockSpec(memory_space=pl.ANY)
    a_full = jax.ShapeDtypeStruct((steps, 4, 2, al.shape[1], width), BF16)
    b_full = jax.ShapeDtypeStruct((steps, 2, 4, 4, bl.shape[1], width), BF16)
    out = pl.pallas_call(
        gather_kernel,
        out_shape=[a_full, a_full, b_full, b_full],
        in_specs=[hbm] * 4,
        out_specs=[hbm] * 4,
        scratch_shapes=[
            pltpu.SemaphoreType.DMA((2 * Exchange.COPIES,)),
            pltpu.SemaphoreType.DMA((2 * Exchange.COPIES,)),
            pltpu.SemaphoreType.DMA((8,)),
        ],
        compiler_params=pltpu.CompilerParams(collective_id=0, has_side_effects=True),
    )(al, ar, bl, br)
    return [x.reshape(steps, -1, width) for x in out]


def on_device(c_left, c_right, c_rank, a_left, a_right, a_rank, a_pattern, b_left, b_right, b_rank, b_pattern, probe, target):
    al, ar, bl, br = gather(a_left[0], a_right[0], b_left[:, 0], b_right[:, 0])
    ranks = jnp.concatenate(
        [
            c_rank[0],
            target[0, 0],
            a_rank[0],
            b_rank[:, 0],
            a_pattern[0] * b_pattern[:, 0],
        ]
    )
    left, right = compute(ranks, c_left[0, 0], c_right[0, 0], probe, al, ar, bl, br)
    return left[None, None], right[None, None]


def solution(mesh):
    return jax.shard_map(
        on_device,
        mesh=mesh,
        in_specs=(
            P("row", "col", None, None),
            P("row", "col", None, None),
            P("row", "col"),
            P("row", None, "col", None),
            P("row", None, "col", None),
            P("row", None),
            P("row", None),
            P(None, "col", "row", None),
            P(None, "col", "row", None),
            P(None, "col"),
            P(None, "col"),
            P(),
            P("row", "col", None),
        ),
        out_specs=(P("row", "col", None, None), P("row", "col", None, None)),
        check_vma=False,
    )
```

```python
import functools
import math

import jax
import jax.numpy as jnp
from jax import lax
from jax.experimental import pallas as pl
from jax.experimental.pallas import tpu as pltpu
from jax.sharding import PartitionSpec as P

F32 = jnp.float32
BF16 = jnp.bfloat16
PANEL = 32
CHUNK = 256
TILE = 2048


def split2(x):
    hi = x.astype(BF16)
    return hi, (x - hi.astype(F32)).astype(BF16)


def split3(x):
    hi = x.astype(BF16)
    rest = x - hi.astype(F32)
    mid = rest.astype(BF16)
    return hi, mid, (rest - mid.astype(F32)).astype(BF16)


def mm(a, b):
    return jnp.dot(a, b, preferred_element_type=F32)


def tmm(a, b):
    return lax.dot_general(a, b, (((0,), (0,)), ((), ())), preferred_element_type=F32)


def mmt(a, b):
    return lax.dot_general(a, b, (((1,), (1,)), ((), ())), preferred_element_type=F32)


def times(op, a, b):
    ah, al = split2(a)
    bh, bl = split2(b)
    return op(ah, bh) + (op(ah, bl) + op(al, bh))


def fine(op, a, b):
    a0, a1, a2 = split3(a)
    b0, b1, b2 = split3(b)
    return op(a0, b0) + ((op(a0, b1) + op(a1, b0)) + (op(a1, b1) + (op(a0, b2) + op(a2, b0))))


def lane(x, c):
    return jnp.broadcast_to(x[:, c : c + 1], (8, 128))


def sublane(x, r):
    return jnp.broadcast_to(x[r : r + 1, :], (8, 128))


def panel_step(p, work, inv_ref, beside):
    width = work.shape[1] // 2
    vregs = work.shape[1] // 128
    groups = PANEL // 8
    rows = [
        [work[8 * g : 8 * g + 8, 128 * v : 128 * v + 128] for v in range(vregs)] for g in range(groups)
    ]
    below = pltpu.roll(work[PANEL:width, :width], width - PANEL, 1)
    sub = lax.broadcasted_iota(jnp.int32, (8, 128), 0)
    beside(p)
    for b in range(groups):
        cols = [[lane(rows[g][0], 8 * b + m) for m in range(8)] for g in range(groups)]
        d = [[sublane(cols[b][n], m) for n in range(m + 1)] for m in range(8)]
        heads = [[sublane(rows[b][v], n) for v in range(vregs)] for n in range(8)]
        w = [[None] * 8 for _ in range(8)]
        low = [[None] * 8 for _ in range(8)]
        for k in range(8):
            r = lax.rsqrt(d[k][k])
            w[k][k] = r
            for m in range(k + 1, 8):
                low[m][k] = d[m][k] * r
            for m in range(k + 1, 8):
                for n in range(k + 1, m + 1):
                    d[m][n] = d[m][n] - low[m][k] * low[n][k]
            for n in range(k):
                total = low[k][n] * w[n][n]
                for l in range(n + 1, k):
                    total = total + low[k][l] * w[l][n]
                w[k][n] = -(total * r)
        for v in range(vregs):
            total = None
            for n in range(8):
                column = jnp.zeros((8, 128), F32)
                for m in range(n, 8):
                    column = jnp.where(sub == m, w[m][n], column)
                term = column * heads[n][v]
                total = term if total is None else total + term
            rows[b][v] = total
        for g in range(b + 1, groups):
            heads_u = [[sublane(rows[b][v], m) for v in range(vregs)] for m in range(8)]
            for m in range(8):
                coef = w[m][0] * cols[g][0]
                for l in range(1, m + 1):
                    coef = coef + w[m][l] * cols[g][l]
                for v in range(vregs):
                    rows[g][v] = rows[g][v] - coef * heads_u[m][v]
    upper = jnp.concatenate([jnp.concatenate(rows[g], axis=1) for g in range(groups)], axis=0)
    start = pl.multiple_of(p * PANEL, PANEL)
    inv_ref[pl.ds(start, PANEL), :] = upper[:, width:]
    ahead = pltpu.roll(upper[:, :width], width - PANEL, 1)
    h, m, l = split3(jnp.concatenate([ahead, upper[:, width:]], axis=1))
    hg, mg, lg = h[:, :width], m[:, :width], l[:, :width]
    update = tmm(
        jnp.concatenate([hg, hg, mg, mg, hg, lg], axis=0),
        jnp.concatenate([h, m, h, m, l, h], axis=0),
    )
    rest = width - PANEL
    work[0:rest, width:] = work[PANEL:width, width:] - update[:rest, width:]
    work[0:rest, :width] = below - update[:rest, :width]


def inverse_factor(gram, live, work, inv_ref, between, beside):
    width = gram.shape[0]
    r = lax.broadcasted_iota(jnp.int32, (width, width), 0)
    c = lax.broadcasted_iota(jnp.int32, (width, width), 1)
    eye = jnp.where(r == c, 1.0, 0.0)
    work[:, :width] = gram + eye * (1.0 - live)
    work[:, width:] = eye

    def body(p, carry):
        between(p)
        panel_step(p, work, inv_ref, beside)
        return carry

    lax.fori_loop(0, width // PANEL, body, 0)


class Exchange:
    COPIES = 40

    def __init__(self, k, al_in, ar_in, bl_in, br_in, al, ar, bl, br, send, recv, local):
        self.k = k
        self.send, self.recv, self.local = send, recv, local
        row, col = lax.axis_index("row"), lax.axis_index("col")
        self.x, self.y, self.z = row % 4, (row // 4) % 4, row // 16
        self.h, self.c = col // 2, col % 2
        self.row, self.col = row, col
        self.ins = {"al": al_in, "ar": ar_in, "bl": bl_in, "br": br_in}
        self.full = {"al": al, "ar": ar, "bl": bl, "br": br}
        self.base = k * self.COPIES
        self.offset = {"bl": 0, "br": 11, "ar": 22, "al": 31}

    def at_row(self, x=None, y=None, z=None):
        x = self.x if x is None else x
        y = self.y if y is None else y
        z = self.z if z is None else z
        return ((z * 4 + y) * 4 + x, self.col)

    def at_col(self, h=None, c=None):
        h = self.h if h is None else h
        c = self.c if c is None else c
        return (self.row, h * 2 + c)

    def peers(self):
        yield self.at_row(z=1 - self.z)
        for d in (1, 2, 3):
            yield self.at_row(x=(self.x + d) % 4)
            yield self.at_row(y=(self.y + d) % 4)
        yield self.at_col(h=(self.h + 1) % 4)
        yield self.at_col(h=(self.h + 3) % 4)
        yield self.at_col(c=1 - self.c)

    def copy(self, name, i, src, dst, to):
        n = self.base + self.offset[name] + i
        return pltpu.make_async_remote_copy(
            src_ref=src,
            dst_ref=dst,
            send_sem=self.send.at[n],
            recv_sem=self.recv.at[n],
            device_id=to,
            device_id_type=pl.DeviceIdType.MESH,
        )

    def own(self, name):
        i = ("bl", "br", "ar", "al").index(name)
        src = self.ins[name].at[self.k]
        dst = self.full[name].at[self.k]
        dst = dst.at[self.z, self.y, self.x] if name[0] == "b" else dst.at[self.h, self.c]
        return pltpu.make_async_copy(src, dst, self.local.at[4 * self.k + i])

    def b_pair(self, name):
        src = self.ins[name].at[self.k]
        full = self.full[name].at[self.k]
        return [self.copy(name, 0, src, full.at[self.z, self.y, self.x], self.at_row(z=1 - self.z))]

    def b_near(self, name, second):
        full = self.full[name].at[self.k]
        z = 1 - self.z if second else self.z
        slot = full.at[z, self.y, self.x]
        src = slot if second else self.ins[name].at[self.k]
        out = []
        for d in (1, 2, 3):
            to = self.at_row(x=(self.x + d) % 4) if name == "bl" else self.at_row(y=(self.y + d) % 4)
            out.append(self.copy(name, (3 if second else 0) + d, src, slot, to))
        return out

    def b_line(self, name, place, z=None):
        full = self.full[name].at[self.k]
        if name == "bl":
            return full.at[:, place] if z is None else full.at[z, place]
        return full.at[:, :, place] if z is None else full.at[z, :, place]

    def b_to(self, name, step):
        if name == "bl":
            return self.at_row(y=(self.y + step) % 4)
        return self.at_row(x=(self.x + step) % 4)

    def b_far(self, name):
        here = self.y if name == "bl" else self.x
        line = self.b_line(name, here)
        return [self.copy(name, 7, line, line, self.b_to(name, 1)), self.copy(name, 8, line, line, self.b_to(name, 3))]

    def b_last(self, name):
        here = self.y if name == "bl" else self.x
        back = self.b_line(name, (here + 3) % 4, 0)
        ahead = self.b_line(name, (here + 1) % 4, 1)
        return [self.copy(name, 9, back, back, self.b_to(name, 1)), self.copy(name, 10, ahead, ahead, self.b_to(name, 3))]

    def a_slot(self, name, h, half=None):
        slot = self.full[name].at[self.k].at[h, self.c]
        if half is None:
            return slot
        n = slot.shape[0] // 2
        return slot.at[pl.ds(half * n, n)]

    def a_first(self, name):
        src = self.ins[name].at[self.k]
        slot = self.a_slot(name, self.h)
        return [
            self.copy(name, 0, src, slot, self.at_col(h=(self.h + 1) % 4)),
            self.copy(name, 1, src, slot, self.at_col(h=(self.h + 3) % 4)),
            self.copy(name, 4, src, slot, self.at_col(c=1 - self.c)),
        ]

    def a_second(self, name):
        back = self.a_slot(name, (self.h + 3) % 4, 0)
        ahead = self.a_slot(name, (self.h + 1) % 4, 1)
        return [
            self.copy(name, 2, back, back, self.at_col(h=(self.h + 1) % 4)),
            self.copy(name, 3, ahead, ahead, self.at_col(h=(self.h + 3) % 4)),
        ]

    def a_core(self, name):
        out = []
        for i, d in ((5, 3), (6, 1)):
            slot = self.a_slot(name, (self.h + d) % 4)
            out.append(self.copy(name, i, slot, slot, self.at_col(c=1 - self.c)))
        return out

    def a_core_last(self, name):
        out = []
        for half in (0, 1):
            slot = self.a_slot(name, (self.h + 2) % 4, half)
            out.append(self.copy(name, 7 + half, slot, slot, self.at_col(c=1 - self.c)))
        return out


def start(copies):
    for c in copies:
        c.start()
    return copies


def landed(copies):
    for c in copies:
        c.wait_recv()


def left_here(copies):
    for c in copies:
        c.wait_send()


def greet(exchange):
    barrier = pltpu.get_barrier_semaphore()
    count = 0
    for peer in exchange.peers():
        pl.semaphore_signal(barrier, inc=1, device_id=peer, device_id_type=pl.DeviceIdType.MESH)
        count += 1
    pl.semaphore_wait(barrier, count)


def tile_kernel(
    c_rank,
    target,
    a_rank,
    a_pattern,
    b_rank,
    b_pattern,
    left_in,
    right_in,
    probe_in,
    al_in,
    ar_in,
    bl_in,
    br_in,
    s1h_out,
    s1l_out,
    rr_out,
    w1_out,
    left,
    right,
    probe,
    al,
    ar,
    bl,
    br,
    part,
    rr,
    s0h,
    s0l,
    s1h,
    s1l,
    work,
    inv0,
    inv1,
    ls0_ref,
    as0_ref,
    send,
    recv,
    local,
    io,
):
    tile, width = left.shape
    chunks = tile // CHUNK
    loads = [
        pltpu.make_async_copy(right_in, right, io.at[0]),
        pltpu.make_async_copy(probe_in, probe, io.at[1]),
        pltpu.make_async_copy(left_in, left, io.at[2]),
    ]
    start(loads)
    e0, e1 = [Exchange(k, al_in, ar_in, bl_in, br_in, al, ar, bl, br, send, recv, local) for k in range(2)]
    owns = [e.own(n) for e in (e0, e1) for n in ("bl", "br", "ar", "al")]
    start(owns)
    greet(e0)

    lanes = lax.broadcasted_iota(jnp.int32, (1, width), 1)
    subs = lax.broadcasted_iota(jnp.int32, (width, 1), 0)

    def row_mask(count):
        return jnp.where(subs < count, 1.0, 0.0).astype(F32)

    def lane_mask(count):
        return jnp.where(lanes < count, 1.0, 0.0).astype(F32)

    keep = row_mask(c_rank[0, 0])
    live0, live1 = lane_mask(target[0, 0]), lane_mask(target[0, 1])
    zero = jnp.zeros((width, width), F32)

    def at(i):
        return pl.ds(pl.multiple_of(i * CHUNK, CHUNK), CHUNK)

    def a_chunk(ref, k, i):
        return ref[k, i // 2, i % 2]

    def b_chunk(ref, k, i):
        return ref[k, i // 4, i % 4].reshape(CHUNK, width)

    def send_first(e):
        for n in ("bl", "br"):
            start(e.b_pair(n))
        for n in ("bl", "br"):
            start(e.b_near(n, False))
        for n in ("ar", "al"):
            start(e.a_first(n))

    def send_near(e):
        for n in ("bl", "br"):
            landed(e.b_pair(n))
            start(e.b_near(n, True))

    def send_far(e):
        for n in ("bl", "br"):
            landed(e.b_near(n, False))
            landed(e.b_near(n, True))
            start(e.b_far(n))

    def send_last(e):
        for n in ("bl", "br"):
            landed(e.b_far(n))
            start(e.b_last(n))

    def send_second(e, n):
        landed(e.a_first(n))
        start(e.a_second(n))
        start(e.a_core(n))

    def send_core(e, n):
        landed(e.a_second(n))
        start(e.a_core_last(n))

    def have_b(e):
        for n in ("bl", "br"):
            landed(e.b_last(n))

    def have_a(e, n):
        landed(e.a_core(n))
        landed(e.a_core_last(n))

    for c in owns:
        c.wait()
    send_first(e0)
    loads[0].wait()
    loads[1].wait()

    def before(i, carry):
        rp0, rp1 = carry
        rh, rl = split2(right[at(i), :])
        p0, p1 = probe[0, at(i), :], probe[1, at(i), :]
        return rp0 + (tmm(rh, p0) + tmm(rl, p0)), rp1 + (tmm(rh, p1) + tmm(rl, p1))

    rps = lax.fori_loop(0, 3, before, (zero, zero))
    send_near(e0)
    core0, rp1 = lax.fori_loop(3, chunks, before, rps)
    core0 = core0 * keep * live0
    rp1 = rp1 * keep
    core0h, core0l = split2(core0)
    send_far(e0)
    send_second(e0, "ar")
    loads[2].wait()

    def partly(i, carry):
        lh, ll = split2(left[at(i), :])
        part[at(i), :] = mm(lh, core0h) + (mm(lh, core0l) + mm(ll, core0h))
        return carry

    lax.fori_loop(0, chunks, partly, 0)
    send_second(e0, "al")
    send_last(e0)
    send_first(e1)
    send_core(e0, "ar")
    have_b(e0)

    def probed(i, carry):
        b00, b01 = carry
        x0 = b_chunk(br, 0, i)
        return b00 + tmm(x0, probe[0, at(i), :]), b01 + tmm(x0, probe[1, at(i), :])

    b00, b01 = lax.fori_loop(0, chunks, probed, (zero, zero))
    have_a(e0, "ar")

    def middles(i, total):
        return total + tmm(a_chunk(ar, 0, i), b_chunk(bl, 0, i))

    mid0 = lax.fori_loop(0, chunks, middles, zero)
    weight0 = (a_pattern[0, 0] * b_pattern[0, 0]).astype(F32)
    weight1 = (a_pattern[0, 1] * b_pattern[1, 0]).astype(F32)
    mid0 = mid0 * row_mask(a_rank[0, 0]) * lane_mask(b_rank[0, 0]) * weight0
    sc0 = fine(mm, mid0, b00) * live0
    mb0 = fine(mm, mid0, b01)
    sc0h, sc0l = split2(sc0)
    send_near(e1)
    send_core(e0, "al")
    have_a(e0, "al")

    def first(i, carry):
        gh, gx, gl = carry
        a = a_chunk(al, 0, i)
        s = part[at(i), :] + (mm(a, sc0h) + mm(a, sc0l))
        sh, sl = split2(s)
        s0h[at(i), :] = sh
        s0l[at(i), :] = sl
        return gh + tmm(sh, sh), gx + tmm(sh, sl), gl + tmm(sl, sl)

    gh, gx, gl = lax.fori_loop(0, chunks, first, (zero,) * 3)
    ls0_ref[...] = zero
    as0_ref[...] = zero
    send_far(e1)
    send_second(e1, "ar")

    def between0(p):
        @pl.when(p == 1)
        def _():
            send_second(e1, "al")

        @pl.when(p == 2)
        def _():
            send_last(e1)
            send_core(e1, "ar")

        @pl.when(p == 4)
        def _():
            send_core(e1, "al")

    def beside0(p):
        lh, ll = split2(left[at(p), :])
        sh, sl = s0h[at(p), :], s0l[at(p), :]
        a = a_chunk(al, 0, p)
        ls0_ref[...] += tmm(lh, sh) + (tmm(lh, sl) + tmm(ll, sh))
        as0_ref[...] += tmm(a, sh) + tmm(a, sl)

    inverse_factor(gh + (gx + gx.T) + gl, live0, work, inv0, between0, beside0)
    w0, ls0, as0 = inv0[...], ls0_ref[...], as0_ref[...]
    have_b(e1)
    have_a(e1, "ar")
    have_a(e1, "al")

    def cores(i, carry):
        mid, b11 = carry
        return (
            mid + tmm(a_chunk(ar, 1, i), b_chunk(bl, 1, i)),
            b11 + tmm(b_chunk(br, 1, i), probe[1, at(i), :]),
        )

    mid1, b11 = lax.fori_loop(0, chunks, cores, (zero, zero))
    mid1 = mid1 * row_mask(a_rank[0, 1]) * lane_mask(b_rank[1, 0]) * weight1
    sc1 = fine(mm, mid1, b11) * live1
    y = fine(tmm, ls0, rp1) + fine(tmm, as0, mb0)
    z = fine(tmm, w0, fine(mm, w0, y)) * live1
    zh, zl = split2(z)
    sc1h, sc1l = split2(sc1)

    def second(i, carry):
        gh, gx, gl, ss, as_ = carry
        a = a_chunk(al, 1, i)
        ph, pl_ = s0h[at(i), :], s0l[at(i), :]
        s = (mm(ph, zh) + (mm(ph, zl) + mm(pl_, zh))) + (mm(a, sc1h) + mm(a, sc1l))
        sh, sl = split2(s)
        s1h[at(i), :] = sh
        s1l[at(i), :] = sl
        return (
            gh + tmm(sh, sh),
            gx + tmm(sh, sl),
            gl + tmm(sl, sl),
            ss + (tmm(ph, sh) + (tmm(ph, sl) + tmm(pl_, sh))),
            as_ + (tmm(a, sh) + tmm(a, sl)),
        )

    gh, gx, gl, ss, as1 = lax.fori_loop(0, chunks, second, (zero,) * 5)
    stores = [
        pltpu.make_async_copy(s1h, s1h_out, io.at[0]),
        pltpu.make_async_copy(s1l, s1l_out, io.at[1]),
        pltpu.make_async_copy(rr, rr_out, io.at[2]),
    ]
    start(stores[:2])
    turn = fine(mm, w0, ss)
    tr = fine(mm, fine(mmt, ls0, w0) * keep, turn)
    tb0 = fine(tmm, mid0, fine(mm, fine(mmt, as0, w0), turn))
    tb1 = fine(tmm, mid1, as1)
    trh, trl = split2(tr)
    tb0h, tb0l = split2(tb0)
    tb1h, tb1l = split2(tb1)

    def beside1(p):
        rh, rl = split2(right[at(p), :])
        x0, x1 = b_chunk(br, 0, p), b_chunk(br, 1, p)
        rr[at(p), :] = (mm(rh, trh) + (mm(rh, trl) + mm(rl, trh))) + (
            (mm(x0, tb0h) + mm(x0, tb0l)) + (mm(x1, tb1h) + mm(x1, tb1l))
        )

    inverse_factor(gh + (gx + gx.T) + gl, live1, work, inv1, lambda p: None, beside1)
    start(stores[2:])
    w1_out[...] = inv1[...]
    for e in (e0, e1):
        for n in ("bl", "br"):
            for copies in (e.b_pair(n), e.b_near(n, False), e.b_near(n, True), e.b_far(n), e.b_last(n)):
                left_here(copies)
        for n in ("ar", "al"):
            for copies in (e.a_first(n), e.a_second(n), e.a_core(n), e.a_core_last(n)):
                left_here(copies)
    for c in stores:
        c.wait()


def update(c_rank, target, a_rank, a_pattern, b_rank, b_pattern, left, right, probe, al, ar, bl, br):
    tile, width = left.shape
    steps = probe.shape[0]
    rows = al.shape[1]
    vmem = pl.BlockSpec(memory_space=pltpu.VMEM)
    smem = pl.BlockSpec(memory_space=pltpu.SMEM)
    hbm = pl.BlockSpec(memory_space=pl.ANY)
    a_full = pltpu.VMEM((steps, 4, 2, rows, width), BF16)
    b_full = pltpu.VMEM((steps, 2, 4, 4, bl.shape[1], width), BF16)
    square = pltpu.VMEM((width, width), F32)
    return pl.pallas_call(
        tile_kernel,
        out_shape=[
            jax.ShapeDtypeStruct((tile, width), BF16),
            jax.ShapeDtypeStruct((tile, width), BF16),
            jax.ShapeDtypeStruct((tile, width), F32),
            jax.ShapeDtypeStruct((width, width), F32),
        ],
        in_specs=[smem] * 6 + [hbm] * 3 + [vmem] * 4,
        out_specs=[hbm] * 3 + [vmem],
        scratch_shapes=[
            pltpu.VMEM((tile, width), F32),
            pltpu.VMEM((tile, width), F32),
            pltpu.VMEM((steps, tile, width), BF16),
            a_full,
            a_full,
            b_full,
            b_full,
            pltpu.VMEM((tile, width), F32),
            pltpu.VMEM((tile, width), F32),
        ]
        + [pltpu.VMEM((tile, width), BF16)] * 4
        + [pltpu.VMEM((width, 2 * width), F32)]
        + [square] * 4
        + [
            pltpu.SemaphoreType.DMA((2 * Exchange.COPIES,)),
            pltpu.SemaphoreType.DMA((2 * Exchange.COPIES,)),
            pltpu.SemaphoreType.DMA((8,)),
            pltpu.SemaphoreType.DMA((3,)),
        ],
        compiler_params=pltpu.CompilerParams(
            collective_id=0, has_side_effects=True, vmem_limit_bytes=60 * 1024 * 1024
        ),
    )(c_rank, target, a_rank, a_pattern, b_rank, b_pattern, left, right, probe, al, ar, bl, br)


def finish_kernel(w1, sh, sl, rr, out_left, out_right, wh, wl):
    root = math.sqrt(TILE)

    @pl.when(pl.program_id(0) == 0)
    def _():
        h, l = split2(w1[...])
        wh[...] = h
        wl[...] = l

    h, l = wh[...], wl[...]
    out_left[...] = (mmt(sh[...], h) + (mmt(sh[...], l) + mmt(sl[...], h))) * root
    rh, rl = split2(rr[...])
    out_right[...] = (mmt(rh, h) + (mmt(rh, l) + mmt(rl, h))) * (1.0 / root)


def finish(w1, sh, sl, rr):
    tile, width = rr.shape
    block = pl.BlockSpec((CHUNK, width), lambda i: (i, 0))
    return pl.pallas_call(
        finish_kernel,
        grid=(tile // CHUNK,),
        out_shape=[jax.ShapeDtypeStruct((tile, width), F32)] * 2,
        in_specs=[pl.BlockSpec((width, width), lambda i: (0, 0)), block, block, block],
        out_specs=[block, block],
        scratch_shapes=[pltpu.VMEM((width, width), BF16)] * 2,
    )(w1, sh, sl, rr)


def on_device(c_left, c_right, c_rank, a_left, a_right, a_rank, a_pattern, b_left, b_right, b_rank, b_pattern, probe, target):
    sh, sl, rr, w1 = update(
        c_rank,
        target[0],
        a_rank,
        a_pattern,
        b_rank,
        b_pattern,
        c_left[0, 0],
        c_right[0, 0],
        probe,
        a_left[0],
        a_right[0],
        b_left[:, 0],
        b_right[:, 0],
    )
    left, right = finish(w1, sh, sl, rr)
    return left[None, None], right[None, None]


def solution(mesh):
    return jax.shard_map(
        on_device,
        mesh=mesh,
        in_specs=(
            P("row", "col", None, None),
            P("row", "col", None, None),
            P("row", "col"),
            P("row", None, "col", None),
            P("row", None, "col", None),
            P("row", None),
            P("row", None),
            P(None, "col", "row", None),
            P(None, "col", "row", None),
            P(None, "col"),
            P(None, "col"),
            P(),
            P("row", "col", None),
        ),
        out_specs=(P("row", "col", None, None), P("row", "col", None, None)),
        check_vma=False,
    )
```
